32 devices in a mesh: aa: 8 (over y, x, core), ba: 4 (over z).
Axes of the slice: x: 2, y: 2, z: 4, core: 2. Of those that a mesh axis runs over, the one named last changes fastest.
Arguments:
- fast_query: bfloat16 [2, 2048, 5120], P(None, 'aa', 'ba'), may hold values from -6 to 6
- fast_key: bfloat16 [2, 2048, 5120], P(None, 'aa', 'ba'), may hold values from -6 to 6
- fast_value: bfloat16 [2, 2048, 5120], P(None, 'aa', 'ba'), may hold values from -6 to 6
- rates: float32 [2, 2048, 24], P(None, 'aa', 'ba'), may hold values from 5e-05 to 0.0005
- attn_query: bfloat16 [2, 2048, 5120], P(None, 'aa', 'ba'), may hold values from -4.5 to 4.5
- attn_key: bfloat16 [2, 2048, 5120], P(None, 'aa', 'ba'), may hold values from -4.5 to 4.5
- attn_value: bfloat16 [2, 2048, 5120], P(None, 'aa', 'ba'), may hold values from -6 to 6
- fast_weights: float32 [640, 3, 8, 640], P('aa', None, 'ba'), may hold values from -0.2814427 to 0.2814427
- gain: float32 [5120], replicated, may hold values from 0.5 to 1.5
Outputs:
- mixed: bfloat16 [2, 2048, 5120], P(None, ('aa', 'ba'))
- weights_out: float32 [640, 3, 8, 640], P('aa', None, 'ba')
- moment_out: float32 [640, 3, 8, 640], P('aa', None, 'ba')
The draws below stay inside these ranges and needn't reach their ends.
All inputs are finite; a program needn't handle non-finite values.
Results may differ from the reference program's by a relative error of at most 0.028.
Values may be sent and summed in bfloat16 or wider, within the bound.
A program may use at most 192 MiB of HBM per device.

```python
import math
import jax
import jax.numpy as jnp
from jax import lax

H = 8
DH = 640
FH = 640
AH = 40
AD = 128
WINDOW = 512
STRETCHES = 2
TOK_DEV = 256
TOKENS = 2048
N_AA = 8


def attention_pair(key):
    base = jax.random.fold_in(key, 7)
    key_q, key_k = jax.random.split(base, 2)
    shape = (STRETCHES, TOKENS, AH * AD)
    query = jnp.clip(jax.random.normal(key_q, shape, jnp.float32), -4.5, 4.5)
    keys = jnp.clip(jax.random.normal(key_k, shape, jnp.float32), -4.5, 4.5)
    return (query, keys)


def draw_attn_query(key, part):
    query, keys = attention_pair(key)
    return query.astype(jnp.bfloat16)


def draw_attn_key(key, part):
    query, keys = attention_pair(key)
    return keys.astype(jnp.bfloat16)


def draw_fast_weights(key, part):
    key_b, key_c = jax.random.split(jax.random.fold_in(key, 11), 2)
    shape = (FH, 3, H, DH)
    base = jnp.clip(jax.random.normal(key_b, shape, jnp.float32), -4.0, 4.0)
    cols = jnp.exp(jax.random.uniform(key_c, (3, H, DH), jnp.float32, 0.0, math.log(10.0)))
    return base * cols[None] * (8.0 / (45.0 * math.sqrt(DH)))


def levels(rng, shape, shards, least, top_value):
    factor_of = 1.0
    for position, parts in shards:
        steps = jax.random.uniform(jax.random.fold_in(jax.random.fold_in(rng, 6), position), (parts,), jnp.float32, least / len(shards), top_value / len(shards))
        factor_of = factor_of * jnp.repeat(jnp.exp(steps), shape[position] // parts).reshape((-1,) + (1,) * (len(shape) - 1 - position))
    return factor_of


def bell_draw(key, dims, scale, most, shards=(), held_as=jnp.bfloat16):
    values = scale * jax.random.normal(key, dims, jnp.float32)
    if shards:
        values = values * levels(key, dims, shards, -0.22, 0.18)
    return jnp.clip(values, -most, most).astype(held_as)


def setup_inputs(seed: int = 0) -> dict:
    splits = jax.random.split(jax.random.key(seed), 10)
    fast_query = bell_draw(splits[0], (STRETCHES, TOKENS, H * DH), 1.0, 6.0, ((1, 8), (2, 4)))
    fast_key = bell_draw(splits[1], (STRETCHES, TOKENS, H * DH), 1.0, 6.0, ((1, 8), (2, 4)))
    fast_value = bell_draw(splits[2], (STRETCHES, TOKENS, H * DH), 1.0, 6.0, ((1, 8), (2, 4)))
    rates = jnp.clip(jnp.exp(math.log(0.0005) - 2.3025852 * jax.random.uniform(splits[3], (STRETCHES, TOKENS, 3 * H), jnp.float32) ** levels(splits[3], (STRETCHES, TOKENS, 3 * H), ((1, 8), (2, 4)), -0.2, 0.2)), 4.999999873689376e-05, 0.0005)
    attn_query = draw_attn_query(jax.random.fold_in(splits[9], 71), 0)
    attn_key = draw_attn_key(jax.random.fold_in(splits[9], 71), 0)
    attn_value = bell_draw(splits[6], (STRETCHES, TOKENS, AH * AD), 1.0, 6.0, ((1, 8), (2, 4)))
    fast_weights = draw_fast_weights(jax.random.fold_in(splits[9], 71), 0)
    gain = jnp.clip(1.0 + 0.1 * jax.random.normal(splits[8], (H * DH,), jnp.float32), 0.5, 1.5)
    return {"fast_query": fast_query, "fast_key": fast_key, "fast_value": fast_value, "rates": rates, "attn_query": attn_query, "attn_key": attn_key, "attn_value": attn_value, "fast_weights": fast_weights, "gain": gain}


BETA = 0.9
EPS = 1e-06

def activation(x):
    sig = jax.nn.sigmoid(x)
    return (x * sig, sig * (1.0 + x * (1.0 - sig)))

def project(x, w):
    return jnp.einsum('nhd,fhd->nhf', x.astype(jnp.float32), w.astype(jnp.float32))

def fast_stretch(weights, query, key, value, rate):
    tokens = query.shape[0]
    wbf = weights.astype(jnp.bfloat16)
    q = query.reshape(tokens, H, DH)
    k = key.reshape(tokens, H, DH)
    v = value.reshape(tokens, H, DH)
    act_q, slope_q = activation(project(q, wbf[:, 0]))
    hidden_q = (act_q * project(q, wbf[:, 1])).astype(jnp.bfloat16)
    out = jnp.einsum('nhf,fhd->nhd', hidden_q.astype(jnp.float32), wbf[:, 2].astype(jnp.float32)).reshape(tokens, H * DH)
    gate_in = project(k, wbf[:, 0])
    up_in = project(k, wbf[:, 1])
    back_in = project(v, wbf[:, 2])
    act, slope = activation(gate_in)
    rate = rate.reshape(tokens, H, 3)
    gate_x = (rate[..., 0:1] * (-back_in * up_in * slope)).astype(jnp.bfloat16)
    up_x = (rate[..., 1:2] * (-back_in * act)).astype(jnp.bfloat16)
    down_x = (rate[..., 2:3] * -(act * up_in)).astype(jnp.bfloat16)

    def block(total, index):
        start = index * TOK_DEV

        def cut(x):
            return lax.dynamic_slice_in_dim(x, start, TOK_DEV, 0).astype(jnp.float32)
        gate_g = jnp.einsum('nhf,nhd->fhd', cut(gate_x), cut(k))
        up_g = jnp.einsum('nhf,nhd->fhd', cut(up_x), cut(k))
        down_g = jnp.einsum('nhf,nhd->fhd', cut(down_x), cut(v))
        stacked = jnp.stack([gate_g, up_g, down_g], 1)
        rounded = lax.optimization_barrier(stacked.astype(jnp.bfloat16))
        return (total + rounded.astype(jnp.float32), None)
    grads, unused = lax.scan(block, jnp.zeros((FH, 3, H, DH), jnp.float32), jnp.arange(N_AA, dtype=jnp.int32))
    return (out, grads)

def renorm(trial, target):
    return trial * (target / jnp.sqrt(lax.optimization_barrier(jnp.sum(trial * trial, 0)) + EPS))

def attend(query, key, value):
    total = STRETCHES * TOKENS
    q = query.reshape(total, AH, AD)
    k = key.reshape(total, AH, AD)
    v = value.reshape(total, AH, AD)
    reach = (WINDOW - 2) // TOK_DEV + 1
    margin = reach * TOK_DEV
    k_pad = jnp.concatenate([jnp.zeros((margin, AH, AD), k.dtype), k], 0)
    v_pad = jnp.concatenate([jnp.zeros((margin, AH, AD), v.dtype), v], 0)

    def block(index):
        start = index * TOK_DEV
        q_blk = lax.dynamic_slice_in_dim(q, start, TOK_DEV, 0).astype(jnp.float32)
        k_blk = lax.dynamic_slice_in_dim(k_pad, start, margin + TOK_DEV, 0).astype(jnp.float32)
        v_blk = lax.dynamic_slice_in_dim(v_pad, start, margin + TOK_DEV, 0).astype(jnp.float32)
        scores = jnp.einsum('qhe,khe->hqk', q_blk, k_blk) / math.sqrt(AD)
        q_pos = start + jnp.arange(TOK_DEV, dtype=jnp.int32)
        k_pos = start - margin + jnp.arange(margin + TOK_DEV, dtype=jnp.int32)
        mask = (k_pos[None, :] <= q_pos[:, None]) & (k_pos[None, :] > q_pos[:, None] - WINDOW) & (k_pos[None, :] >= 0)
        scores = jnp.where(mask[None], scores, -1e+30)
        top = lax.optimization_barrier(jnp.max(scores, -1, keepdims=True))
        probs = jnp.exp(scores - top)
        denom = lax.optimization_barrier(jnp.sum(probs, -1))
        rounded = lax.optimization_barrier(probs.astype(jnp.bfloat16)).astype(jnp.float32)
        out = jnp.einsum('hqk,khe->qhe', rounded, v_blk)
        return out / jnp.transpose(denom)[:, :, None]
    outs = lax.map(block, jnp.arange(total // TOK_DEV, dtype=jnp.int32))
    return outs.reshape(STRETCHES, TOKENS, AH * AD)

def reference(fast_query, fast_key, fast_value, rates, attn_query, attn_key, attn_value, fast_weights, gain):
    target = jnp.sqrt(lax.optimization_barrier(jnp.sum(fast_weights * fast_weights, 0)) + EPS)
    weights = fast_weights
    moment = jnp.zeros_like(fast_weights)
    fast_out = []
    for stretch in range(STRETCHES):
        out, grads = fast_stretch(weights, fast_query[stretch], fast_key[stretch], fast_value[stretch], rates[stretch])
        fast_out.append(out)
        moment = BETA * moment + grads
        weights = renorm(weights - moment, target)
    attention = attend(attn_query, attn_key, attn_value)
    combined = lax.optimization_barrier((jnp.stack(fast_out) + attention).astype(jnp.bfloat16)).astype(jnp.float32)
    scale = lax.rsqrt(lax.optimization_barrier(jnp.mean(combined * combined, -1, keepdims=True)) + EPS)
    mixed = (combined * scale * gain).astype(jnp.bfloat16)
    return (mixed, weights, moment)
```

```python
import functools
import math

import jax
import jax.numpy as jnp
from jax import lax
from jax.experimental import pallas as pl
from jax.experimental.pallas import tpu as pltpu
from jax.sharding import PartitionSpec as P

AD = 128
WINDOW = 512


BETA = 0.9
EPS = 1e-06


def shift(x, axis, by):
    length = lax.axis_size(axis)
    return lax.ppermute(x, axis, [(i, (i + by) % length) for i in range(length)])


def activation(x):
    sig = jax.nn.sigmoid(x)
    return (x * sig, sig * (1.0 + x * (1.0 - sig)))


def project(x, w):
    return jnp.einsum("nhd,hfd->nhf", x, w, preferred_element_type=jnp.float32)


def forward(w, query):
    rows, heads = query.shape[0], w.shape[1]
    q = query.reshape(rows, heads, -1)
    act_q, _ = activation(project(q, w[0]))
    hidden_q = (act_q * project(q, w[1])).astype(jnp.bfloat16)
    return jnp.einsum("nhf,hfd->nhd", hidden_q, w[2], preferred_element_type=jnp.float32).reshape(
        rows, -1
    )


def partial_grads(w, key, value, rate):
    rows, heads = key.shape[0], w.shape[1]
    k = key.reshape(rows, heads, -1)
    v = value.reshape(rows, heads, -1)
    gate_in = project(k, w[0])
    up_in = project(k, w[1])
    back_in = project(v, w[2])
    act, slope = activation(gate_in)
    gate_x = (rate[..., 0:1] * (-back_in * up_in * slope)).astype(jnp.bfloat16)
    up_x = (rate[..., 1:2] * (-back_in * act)).astype(jnp.bfloat16)
    down_x = (rate[..., 2:3] * -(act * up_in)).astype(jnp.bfloat16)

    def part(left, right):
        return jnp.einsum("nhf,nhd->hfd", left, right, preferred_element_type=jnp.float32)

    return jnp.stack([part(gate_x, k), part(up_x, k), part(down_x, v)]).astype(jnp.bfloat16)


def attend_kernel(rows, groups, q_ref, *refs):
    out_ref = refs[-1]
    stretch = pl.program_id(0)
    base = stretch * (rows * groups) + lax.axis_index("aa") * rows
    q = q_ref[0]
    scores = []
    blocks = (len(refs) - 1) // 2
    row = lax.broadcasted_iota(jnp.int32, (rows, rows), 0)
    col = lax.broadcasted_iota(jnp.int32, (rows, rows), 1)
    for back in range(blocks):
        s = lax.dot_general(
            q, refs[back][0], (((1,), (1,)), ((), ())), preferred_element_type=jnp.float32
        ) / math.sqrt(AD)
        gap = row - col + back * rows
        ok = (gap >= 0) & (gap < WINDOW) & (col >= back * rows - base)
        scores.append(jnp.where(ok, s, -1e30))
    top = functools.reduce(jnp.maximum, [jnp.max(s, -1, keepdims=True) for s in scores])
    total = 0.0
    acc = 0.0
    for back in range(blocks):
        p = jnp.exp(scores[back] - top)
        total = total + jnp.sum(p, -1, keepdims=True)
        acc = acc + jnp.dot(
            p.astype(jnp.bfloat16), refs[blocks + back][0], preferred_element_type=jnp.float32
        )
    out_ref[0] = acc / total


def attend(q, keys, values):
    stretches, rows, width = q.shape
    groups = lax.axis_size("aa")
    own = pl.BlockSpec((1, rows, AD), lambda s, h: (s, 0, h))
    index = lax.axis_index("aa")

    def moved(x, back):
        if not back:
            return x
        return jnp.where(index < back, jnp.concatenate([x[:1], x[:-1]], 0), x)

    keys = [moved(x, b) for b, x in enumerate(keys)]
    values = [moved(x, b) for b, x in enumerate(values)]
    return pl.pallas_call(
        functools.partial(attend_kernel, rows, groups),
        grid=(stretches, width // AD),
        in_specs=[own] * (1 + 2 * len(keys)),
        out_specs=own,
        out_shape=jax.ShapeDtypeStruct(q.shape, jnp.float32),
        cost_estimate=pl.CostEstimate(
            flops=4 * stretches * rows * rows * len(keys) * width,
            bytes_accessed=40 * q.size,
            transcendentals=stretches * rows * rows * len(keys) * width // AD,
        ),
        name="attend",
    )(q, *keys, *values)


def sum_kernel(n, x_ref, out_ref, land, send_sem, recv_sem):
    me = lax.axis_index("aa")
    barrier = pltpu.get_barrier_semaphore()
    for step in range(1, n):
        pl.semaphore_signal(
            barrier,
            inc=1,
            device_id={"aa": lax.rem(me + step, n)},
            device_id_type=pl.DeviceIdType.MESH,
        )
    pl.semaphore_wait(barrier, n - 1)
    copies = []
    for step in range(1, n):
        copy = pltpu.make_async_remote_copy(
            src_ref=x_ref,
            dst_ref=land.at[step],
            send_sem=send_sem.at[step],
            recv_sem=recv_sem.at[step],
            device_id={"aa": lax.rem(me + step, n)},
            device_id_type=pl.DeviceIdType.MESH,
        )
        copy.start()
        copies.append(copy)
    total = x_ref[...]
    for step in range(1, n):
        copies[step - 1].wait_recv()
        total = total + land[step]
    for copy in copies:
        copy.wait_send()
    out_ref[...] = total


def sum_over(x):
    n = lax.axis_size("aa")
    vmem = pl.BlockSpec(memory_space=pltpu.VMEM)
    return pl.pallas_call(
        functools.partial(sum_kernel, n),
        in_specs=[vmem],
        out_specs=vmem,
        out_shape=jax.ShapeDtypeStruct(x.shape, x.dtype),
        scratch_shapes=[
            pltpu.VMEM((n,) + x.shape, x.dtype),
            pltpu.SemaphoreType.DMA((n,)),
            pltpu.SemaphoreType.DMA((n,)),
        ],
        compiler_params=pltpu.CompilerParams(collective_id=1, has_side_effects=True),
        name="sum_over",
    )(x)


def tie(values, anchor):
    out = lax.optimization_barrier(tuple(values) + (anchor,))
    return out[:-1], out[-1]


def local(
    fast_query, fast_key, fast_value, rates, attn_query, attn_key, attn_value, fast_weights, gain
):
    stretches, rows, width = fast_query.shape
    local_rows = fast_weights.shape[0]
    heads = fast_weights.shape[2]
    rate = rates.reshape(stretches, rows, heads, 3)
    index = lax.axis_index("aa")
    groups = lax.axis_size("aa")
    first_row = index * local_rows

    shard = jnp.transpose(fast_weights, (1, 2, 0, 3))
    wb = lax.all_gather(shard.astype(jnp.bfloat16), "aa", axis=2, tiled=True)
    (attn_key, attn_value), wb = tie((attn_key, attn_value), wb)
    far = [shift(attn_key, "aa", 2), shift(attn_value, "aa", 2)]

    full = wb.astype(jnp.float32)
    target = jnp.sqrt(jnp.sum(full * full, 2, keepdims=True) + EPS)
    gp = partial_grads(wb, fast_key[0], fast_value[0], rate[0])
    grads = lax.psum(gp, "aa").astype(jnp.float32)

    (fq,), _ = tie((fast_query,), gp)
    out0 = forward(wb, fq[0])
    far, out0 = tie(far, out0)
    odd = index % 2 == 1
    swap = [(i, i ^ 1) for i in range(groups)]
    near = [
        lax.ppermute(jnp.where(odd, f, o), "aa", swap) for f, o in zip(far, (attn_key, attn_value))
    ]
    attention = attend(
        attn_query, [attn_key, near[0], far[0]], [attn_value, near[1], far[1]]
    )
    (attention,), grads = tie((attention,), grads)

    trial = full - grads
    updated = trial * (target / jnp.sqrt(jnp.sum(trial * trial, 2, keepdims=True) + EPS))
    ub = updated.astype(jnp.bfloat16)
    gp1 = partial_grads(ub, fast_key[1], fast_value[1], rate[1])
    grads1 = lax.psum_scatter(gp1, "aa", scatter_dimension=2, tiled=True).astype(jnp.float32)
    (fq1,), _ = tie((fast_query,), gp1)
    out1 = forward(ub, fq1[1])
    combined = (jnp.stack([out0, out1]) + attention).astype(jnp.bfloat16)

    moment = BETA * lax.dynamic_slice_in_dim(grads, first_row, local_rows, 2) + grads1
    own = lax.dynamic_slice_in_dim(updated, first_row, local_rows, 2)
    trial = own - moment
    squares = sum_over(jnp.sum(trial * trial, 2).reshape(-1, trial.shape[3]))
    squares = squares.reshape(trial.shape[:2] + (1, trial.shape[3]))
    weights = trial * (target / jnp.sqrt(squares + EPS))

    arrived = lax.all_to_all(combined, "ba", split_axis=1, concat_axis=2, tiled=True)
    values = arrived.astype(jnp.float32)
    scale = lax.rsqrt(jnp.mean(values * values, -1, keepdims=True) + EPS)
    mixed = (values * scale * gain).astype(jnp.bfloat16)
    back = (2, 0, 1, 3)
    return (mixed, jnp.transpose(weights, back), jnp.transpose(moment, back))


def solution(mesh):
    token = P(None, "aa", "ba")
    hidden = P("aa", None, "ba", None)
    return jax.shard_map(
        local,
        mesh=mesh,
        in_specs=(token,) * 7 + (hidden, P()),
        out_specs=(P(None, ("aa", "ba"), None), hidden, hidden),
        check_vma=False,
    )
```

```python
import functools
import math

import jax
import jax.numpy as jnp
from jax import lax
from jax.experimental import pallas as pl
from jax.experimental.pallas import tpu as pltpu
from jax.sharding import PartitionSpec as P

AD = 128
WINDOW = 512


BETA = 0.9
EPS = 1e-06


def shift(x, axis, by):
    length = lax.axis_size(axis)
    return lax.ppermute(x, axis, [(i, (i + by) % length) for i in range(length)])


def activation(x):
    sig = jax.nn.sigmoid(x)
    return (x * sig, sig * (1.0 + x * (1.0 - sig)))


def project(x, w):
    return jnp.einsum("nhd,hfd->nhf", x, w, preferred_element_type=jnp.float32)


def forward(w, query):
    rows, heads = query.shape[0], w.shape[1]
    q = query.reshape(rows, heads, -1)
    act_q, _ = activation(project(q, w[0]))
    hidden_q = (act_q * project(q, w[1])).astype(jnp.bfloat16)
    return jnp.einsum("nhf,hfd->nhd", hidden_q, w[2], preferred_element_type=jnp.float32).reshape(
        rows, -1
    )


def partial_grads(w, key, value, rate):
    rows, heads = key.shape[0], w.shape[1]
    k = key.reshape(rows, heads, -1)
    v = value.reshape(rows, heads, -1)
    gate_in = project(k, w[0])
    up_in = project(k, w[1])
    back_in = project(v, w[2])
    act, slope = activation(gate_in)
    gate_x = (rate[..., 0:1] * (-back_in * up_in * slope)).astype(jnp.bfloat16)
    up_x = (rate[..., 1:2] * (-back_in * act)).astype(jnp.bfloat16)
    down_x = (rate[..., 2:3] * -(act * up_in)).astype(jnp.bfloat16)

    def part(left, right):
        return jnp.einsum("nhf,nhd->hfd", left, right, preferred_element_type=jnp.float32)

    return jnp.stack([part(gate_x, k), part(up_x, k), part(down_x, v)]).astype(jnp.bfloat16)


def attend_kernel(rows, groups, q_ref, *refs):
    out_ref = refs[-1]
    stretch = pl.program_id(0)
    base = stretch * (rows * groups) + lax.axis_index("aa") * rows
    q = q_ref[0]
    scores = []
    blocks = (len(refs) - 1) // 2
    row = lax.broadcasted_iota(jnp.int32, (rows, rows), 0)
    col = lax.broadcasted_iota(jnp.int32, (rows, rows), 1)
    for back in range(blocks):
        s = lax.dot_general(
            q, refs[back][0], (((1,), (1,)), ((), ())), preferred_element_type=jnp.float32
        ) / math.sqrt(AD)
        gap = row - col + back * rows
        ok = (gap >= 0) & (gap < WINDOW) & (col >= back * rows - base)
        scores.append(jnp.where(ok, s, -1e30))
    top = functools.reduce(jnp.maximum, [jnp.max(s, -1, keepdims=True) for s in scores])
    total = 0.0
    acc = 0.0
    for back in range(blocks):
        p = jnp.exp(scores[back] - top)
        total = total + jnp.sum(p, -1, keepdims=True)
        acc = acc + jnp.dot(
            p.astype(jnp.bfloat16), refs[blocks + back][0], preferred_element_type=jnp.float32
        )
    out_ref[0] = acc / total


def attend(q, keys, values):
    stretches, rows, width = q.shape
    groups = lax.axis_size("aa")
    own = pl.BlockSpec((1, rows, AD), lambda s, h: (s, 0, h))
    index = lax.axis_index("aa")

    def moved(x, back):
        if not back:
            return x
        return jnp.where(index < back, jnp.concatenate([x[:1], x[:-1]], 0), x)

    keys = [moved(x, b) for b, x in enumerate(keys)]
    values = [moved(x, b) for b, x in enumerate(values)]
    return pl.pallas_call(
        functools.partial(attend_kernel, rows, groups),
        grid=(stretches, width // AD),
        in_specs=[own] * (1 + 2 * len(keys)),
        out_specs=own,
        out_shape=jax.ShapeDtypeStruct(q.shape, jnp.float32),
        cost_estimate=pl.CostEstimate(
            flops=4 * stretches * rows * rows * len(keys) * width,
            bytes_accessed=40 * q.size,
            transcendentals=stretches * rows * rows * len(keys) * width // AD,
        ),
        name="attend",
    )(q, *keys, *values)


def sum_kernel(n, x_ref, out_ref, land, send_sem, recv_sem):
    me = lax.axis_index("aa")
    barrier = pltpu.get_barrier_semaphore()
    for step in range(1, n):
        pl.semaphore_signal(
            barrier,
            inc=1,
            device_id={"aa": lax.rem(me + step, n)},
            device_id_type=pl.DeviceIdType.MESH,
        )
    pl.semaphore_wait(barrier, n - 1)
    copies = []
    for step in range(1, n):
        copy = pltpu.make_async_remote_copy(
            src_ref=x_ref,
            dst_ref=land.at[step],
            send_sem=send_sem.at[step],
            recv_sem=recv_sem.at[step],
            device_id={"aa": lax.rem(me + step, n)},
            device_id_type=pl.DeviceIdType.MESH,
        )
        copy.start()
        copies.append(copy)
    total = x_ref[...]
    for step in range(1, n):
        copies[step - 1].wait_recv()
        total = total + land[step]
    for copy in copies:
        copy.wait_send()
    out_ref[...] = total


def sum_over(x):
    n = lax.axis_size("aa")
    vmem = pl.BlockSpec(memory_space=pltpu.VMEM)
    return pl.pallas_call(
        functools.partial(sum_kernel, n),
        in_specs=[vmem],
        out_specs=vmem,
        out_shape=jax.ShapeDtypeStruct(x.shape, x.dtype),
        scratch_shapes=[
            pltpu.VMEM((n,) + x.shape, x.dtype),
            pltpu.SemaphoreType.DMA((n,)),
            pltpu.SemaphoreType.DMA((n,)),
        ],
        compiler_params=pltpu.CompilerParams(collective_id=1, has_side_effects=True),
        name="sum_over",
    )(x)


def tie(values, anchor):
    out = lax.optimization_barrier(tuple(values) + (anchor,))
    return out[:-1], out[-1]


def local(
    fast_query, fast_key, fast_value, rates, attn_query, attn_key, attn_value, fast_weights, gain
):
    stretches, rows, width = fast_query.shape
    local_rows = fast_weights.shape[0]
    heads = fast_weights.shape[2]
    rate = rates.reshape(stretches, rows, heads, 3)
    index = lax.axis_index("aa")
    groups = lax.axis_size("aa")
    first_row = index * local_rows

    shard = jnp.transpose(fast_weights, (1, 2, 0, 3))
    wb = lax.all_gather(shard.astype(jnp.bfloat16), "aa", axis=2, tiled=True)
    (attn_key, attn_value), wb = tie((attn_key, attn_value), wb)
    far = [shift(attn_key, "aa", 2), shift(attn_value, "aa", 2)]

    full = wb.astype(jnp.float32)
    target = jnp.sqrt(jnp.sum(full * full, 2, keepdims=True) + EPS)
    gp = partial_grads(wb, fast_key[0], fast_value[0], rate[0])
    grads = lax.psum(gp, "aa").astype(jnp.float32)

    (fq,), _ = tie((fast_query,), gp)
    out0 = forward(wb, fq[0])
    far, out0 = tie(far, out0)
    odd = index % 2 == 1
    swap = [(i, i ^ 1) for i in range(groups)]
    near = [
        lax.ppermute(jnp.where(odd, f, o), "aa", swap) for f, o in zip(far, (attn_key, attn_value))
    ]
    attention = attend(
        attn_query, [attn_key, near[0], far[0]], [attn_value, near[1], far[1]]
    )
    (attention,), grads = tie((attention,), grads)

    trial = full - grads
    updated = trial * (target / jnp.sqrt(jnp.sum(trial * trial, 2, keepdims=True) + EPS))
    ub = updated.astype(jnp.bfloat16)
    gp1 = partial_grads(ub, fast_key[1], fast_value[1], rate[1])
    grads1 = lax.psum_scatter(gp1, "aa", scatter_dimension=2, tiled=True).astype(jnp.float32)
    (fq1,), _ = tie((fast_query,), gp1)
    out1 = forward(ub, fq1[1])
    combined = (jnp.stack([out0, out1]) + attention).astype(jnp.bfloat16)

    moment = BETA * lax.dynamic_slice_in_dim(grads, first_row, local_rows, 2) + grads1
    own = lax.dynamic_slice_in_dim(updated, first_row, local_rows, 2)
    trial = own - moment
    squares = sum_over(jnp.sum(trial * trial, 2).reshape(-1, trial.shape[3]))
    squares = squares.reshape(trial.shape[:2] + (1, trial.shape[3]))
    weights = trial * (target / jnp.sqrt(squares + EPS))

    arrived = lax.all_to_all(combined, "ba", split_axis=1, concat_axis=2, tiled=True)
    values = arrived.astype(jnp.float32)
    scale = lax.rsqrt(jnp.mean(values * values, -1, keepdims=True) + EPS)
    mixed = (values * scale * gain).astype(jnp.bfloat16)
    back = (2, 0, 1, 3)
    return (mixed, jnp.transpose(weights, back), jnp.transpose(moment, back))


class Comm:
    def __init__(self, send, recv):
        self.send, self.recv, self.used = send, recv, 0
        self.open = []

    def slots(self, count):
        first = self.used
        self.used += count
        return first

    def make(self, slot, src, dst, peer):
        return pltpu.make_async_remote_copy(
            src_ref=src,
            dst_ref=dst,
            send_sem=self.send.at[slot],
            recv_sem=self.recv.at[slot],
            device_id=peer,
            device_id_type=pl.DeviceIdType.MESH,
        )


NT = (((1,), (1,)), ((), ()))
TN = (((0,), (0,)), ((), ()))
NN = (((1,), (0,)), ((), ()))


def mm(a, b, dims):
    return lax.dot_general(a, b, dims, preferred_element_type=jnp.float32)


def block_kernel(
    n,
    parts,
    fq,
    fk,
    fv,
    rate,
    aq,
    ak,
    av,
    wb,
    gain,
    mixed,
    weights,
    moment,
    gp,
    pair,
    sums,
    ring,
    full,
    far,
    near,
    acc,
    comb,
    land,
    target,
    sq,
    sqland,
    send,
    recv,
):
    me = lax.axis_index("aa")
    mine = lax.axis_index("ba")
    group, core = me // 2, lax.rem(me, 2)
    teams = n // 2
    heads = wb.shape[2]
    r, depth = wb.shape[3], wb.shape[4]
    stretches, rows, width = fq.shape
    partner = {"aa": group * 2 + 1 - core}
    comm = Comm(send, recv)

    def peer(step):
        return lax.rem(group + step, teams)

    def source(step):
        return lax.rem(group + teams - step, teams)

    def same(g):
        return {"aa": g * 2 + core}

    barrier = pltpu.get_barrier_semaphore()
    for step in range(1, n):
        pl.semaphore_signal(
            barrier,
            inc=1,
            device_id={"aa": lax.rem(me + step, n)},
            device_id_type=pl.DeviceIdType.MESH,
        )
    for step in range(1, parts):
        pl.semaphore_signal(
            barrier,
            inc=1,
            device_id={"ba": lax.rem(mine + step, parts)},
            device_id_type=pl.DeviceIdType.MESH,
        )
    pl.semaphore_wait(barrier, n + parts - 2)

    pending = []
    halo_first = comm.slots(4 * stretches)
    held = (ak, av)

    def halo(t, s):
        slot = halo_first + t * stretches + s
        copy = comm.make(slot, held[t].at[s], far.at[t, s], same(peer(1)))
        copy.start()
        pending.append(copy)
        return copy

    def swap(t, s):
        slot = halo_first + 2 * stretches + t * stretches + s

        @pl.when(core == 0)
        def _():
            comm.make(slot, held[t].at[s], near.at[t, s], partner).start()

        @pl.when(core == 1)
        def _():
            comm.make(slot, far.at[t, s], near.at[t, s], partner).start()

        copy = comm.make(slot, held[t].at[s], near.at[t, s], partner)
        pending.append(copy)
        return copy

    def whole(ref, m, h):
        return ref[:, m, h].reshape(n * r, depth)

    def grads(ref, s):
        @pl.loop(0, heads)
        def _(h):
            cols = pl.ds(pl.multiple_of(h * depth, 128), depth)
            k = fk[s, :, cols]
            v = fv[s, :, cols]
            gate_in = mm(k, whole(ref, 0, h), NT)
            up_in = mm(k, whole(ref, 1, h), NT)
            back_in = mm(v, whole(ref, 2, h), NT)
            act, slope = activation(gate_in)
            xs = (
                (rate[s, h, 0] * (-back_in * up_in * slope)).astype(jnp.bfloat16),
                (rate[s, h, 1] * (-back_in * act)).astype(jnp.bfloat16),
                (rate[s, h, 2] * -(act * up_in)).astype(jnp.bfloat16),
            )
            for m in range(3):
                part = mm(xs[m], v if m == 2 else k, TN).astype(jnp.bfloat16)
                gp[:, :, m, h] = part.reshape(teams, 2, r, depth)

    def forward(ref, s):
        @pl.loop(0, heads)
        def _(h):
            cols = pl.ds(pl.multiple_of(h * depth, 128), depth)
            q = fq[s, :, cols]
            act, _ = activation(mm(q, whole(ref, 0, h), NT))
            hidden = (act * mm(q, whole(ref, 1, h), NT)).astype(jnp.bfloat16)
            acc[s, :, cols] = mm(hidden, whole(ref, 2, h), NN)

    def attention(s):
        base = s * (rows * n) + me * rows
        places = [s] + [jnp.where(me < b, max(s - 1, 0), s) for b in (1, 2)]
        row = lax.broadcasted_iota(jnp.int32, (rows, rows), 0)
        col = lax.broadcasted_iota(jnp.int32, (rows, rows), 1)
        oks = []
        for back in range(3):
            gap = row - col + back * rows
            oks.append((gap >= 0) & (gap < WINDOW) & (col >= back * rows - base))

        @pl.loop(0, width // AD)
        def _(h):
            cols = pl.ds(pl.multiple_of(h * AD, AD), AD)
            keys = [ak[s, :, cols], near[0, places[1], :, cols], far[0, places[2], :, cols]]
            values = [av[s, :, cols], near[1, places[1], :, cols], far[1, places[2], :, cols]]
            q = aq[s, :, cols]
            scores = [
                jnp.where(ok, mm(q, k, NT) / math.sqrt(AD), -1e30) for ok, k in zip(oks, keys)
            ]
            top = functools.reduce(
                jnp.maximum, [jnp.max(x, -1, keepdims=True) for x in scores]
            )
            total, out = 0.0, 0.0
            for x, v in zip(scores, values):
                p = jnp.exp(x - top)
                total = total + jnp.sum(p, -1, keepdims=True)
                out = out + mm(p.astype(jnp.bfloat16), v, NN)
            comb[s, :, cols] = (acc[s, :, cols] + out / total).astype(jnp.bfloat16)

    def pair_send(phase):
        first = comm.slots(teams)
        copies = []
        for g in range(teams):
            copy = comm.make(first + g, gp.at[g, 1 - core], pair.at[phase, g], partner)
            copy.start()
            copies.append(copy)
        return copies

    def ring_send(phase, copies):
        first = comm.slots(teams)
        for copy in copies:
            copy.wait()
        out = []
        for step in range(1, teams):
            g = peer(step)

            @pl.loop(0, heads)
            def _(h):
                for m in range(3):
                    sums[g, m, h] = (
                        gp[g, core, m, h].astype(jnp.float32)
                        + pair[phase, g, m, h].astype(jnp.float32)
                    ).astype(jnp.bfloat16)

        for step in range(1, teams):
            g = peer(step)
            copy = comm.make(first + step, sums.at[g], ring.at[phase, step], same(g))
            copy.start()
            out.append(copy)
        return out

    def total_of(phase, m, h):
        total = gp[group, core, m, h].astype(jnp.float32) + pair[phase, group, m, h].astype(
            jnp.float32
        )
        for step in range(1, teams):
            total = total + ring[phase, step, m, h].astype(jnp.float32)
        return total

    def exchange(s):
        first = comm.slots(parts)
        chunk = rows // parts
        copies = []
        for step in range(1, parts):
            z = lax.rem(mine + step, parts)
            take = pl.ds(pl.multiple_of(z * chunk, chunk), chunk)
            copy = comm.make(first + step, comb.at[s, take], land.at[s, step], {"ba": z})
            copy.start()
            copies.append(copy)
        return copies

    def finish(s, copies):
        chunk = rows // parts
        take = pl.ds(pl.multiple_of(mine * chunk, chunk), chunk)
        land[s, 0] = comb[s, take]
        for copy in copies:
            copy.wait()
        squares = 0.0
        for step in range(parts):
            x = land[s, step].astype(jnp.float32)
            squares = squares + jnp.sum(x * x, -1, keepdims=True)
        scale = lax.rsqrt(squares / (parts * width) + EPS)
        for step in range(parts):
            z = lax.rem(mine + parts - step, parts)
            cols = pl.ds(pl.multiple_of(z * width, 128), width)
            x = land[s, step].astype(jnp.float32)
            mixed[s, :, cols] = (x * scale * gain[:, cols]).astype(jnp.bfloat16)

    keys0 = halo(0, 0)
    grads(wb, 0)
    copies = pair_send(0)
    forward(wb, 0)
    copies = ring_send(0, copies)
    values0 = halo(1, 0)
    for copy in copies:
        copy.wait()

    @pl.loop(0, heads)
    def _(h):
        for m in range(3):
            full[me, m, h] = total_of(0, m, h).astype(jnp.bfloat16)

    first = comm.slots(2 * teams)
    gathers = []
    for step in range(1, teams):
        copy = comm.make(first + step, full.at[me], full.at[me], same(peer(step)))
        copy.start()
        gathers.append(copy)
    near_copy = comm.make(first + teams, full.at[me], full.at[me], partner)
    near_copy.start()
    later = [halo(t, 1) for t in range(2)]
    keys0.wait_recv()
    values0.wait_recv()
    swaps = [swap(t, 0) for t in range(2)]
    for copy in swaps:
        copy.wait_recv()
    attention(0)
    mixing0 = exchange(0)
    forwards = []
    for step in range(1, teams):
        gathers[step - 1].wait_recv()
        block = source(step) * 2 + core
        copy = comm.make(first + teams + step, full.at[block], full.at[block], partner)
        copy.start()
        forwards.append(copy)
    near_copy.wait()
    for copy in gathers:
        copy.wait_send()
    for copy in forwards:
        copy.wait()

    @pl.loop(0, heads)
    def _(h):
        for m in range(3):
            before, after = 0.0, 0.0
            for j in range(n):
                w = wb[j, m, h].astype(jnp.float32)
                t = w - full[j, m, h].astype(jnp.float32)
                before = before + jnp.sum(w * w, 0, keepdims=True)
                after = after + jnp.sum(t * t, 0, keepdims=True)
            goal = jnp.sqrt(before + EPS)
            target[m, h] = goal
            ratio = goal / jnp.sqrt(after + EPS)
            past = full[me, m, h].astype(jnp.float32)
            moment[m, h] = past
            weights[m, h] = (wb[me, m, h].astype(jnp.float32) - past) * ratio
            for j in range(n):
                w = wb[j, m, h].astype(jnp.float32)
                t = w - full[j, m, h].astype(jnp.float32)
                full[j, m, h] = (t * ratio).astype(jnp.bfloat16)

    grads(full, 1)
    copies = pair_send(1)
    forward(full, 1)
    copies = ring_send(1, copies)
    for copy in later:
        copy.wait_recv()
    swaps = [swap(t, 1) for t in range(2)]
    for copy in swaps:
        copy.wait_recv()
    attention(1)
    mixing1 = exchange(1)
    finish(0, mixing0)
    for copy in copies:
        copy.wait()

    @pl.loop(0, heads)
    def _(h):
        for m in range(3):
            momentum = BETA * moment[m, h] + total_of(1, m, h)
            moment[m, h] = momentum
            trial = weights[m, h] - momentum
            weights[m, h] = trial
            sq[m, h] = jnp.sum(trial * trial, 0, keepdims=True)

    first = comm.slots(n)
    copies = []
    for step in range(1, n):
        copy = comm.make(
            first + step, sq, sqland.at[step], {"aa": lax.rem(me + step, n)}
        )
        copy.start()
        copies.append(copy)
    finish(1, mixing1)
    for copy in copies:
        copy.wait()

    @pl.loop(0, heads)
    def _(h):
        for m in range(3):
            squares = sq[m, h]
            for step in range(1, n):
                squares = squares + sqland[step, m, h]
            weights[m, h] = weights[m, h] * (target[m, h] / jnp.sqrt(squares + EPS))

    for copy in pending:
        copy.wait_send()


def run_blocks(fq, fk, fv, rates, aq, ak, av, wb, gain):
    n, parts = lax.axis_size("aa"), lax.axis_size("ba")
    stretches, rows, width = fq.shape
    heads, r, depth = wb.shape[2:]
    teams = n // 2
    vmem = pl.BlockSpec(memory_space=pltpu.VMEM)
    shard = (3, heads, r, depth)
    small = (3, heads, 1, depth)
    bf, f32 = jnp.bfloat16, jnp.float32
    slots = 4 * stretches + 2 * (2 * teams) + 2 * teams + 2 * parts + n
    return pl.pallas_call(
        functools.partial(block_kernel, n, parts),
        in_specs=[vmem] * 9,
        out_specs=(vmem,) * 3,
        out_shape=(
            jax.ShapeDtypeStruct((stretches, rows // parts, width * parts), bf),
            jax.ShapeDtypeStruct(shard, f32),
            jax.ShapeDtypeStruct(shard, f32),
        ),
        scratch_shapes=[
            pltpu.VMEM((teams, 2) + shard, bf),
            pltpu.VMEM((2, teams) + shard, bf),
            pltpu.VMEM((teams,) + shard, bf),
            pltpu.VMEM((2, teams) + shard, bf),
            pltpu.VMEM((n,) + shard, bf),
            pltpu.VMEM((2, stretches, rows, width), bf),
            pltpu.VMEM((2, stretches, rows, width), bf),
            pltpu.VMEM((stretches, rows, width), f32),
            pltpu.VMEM((stretches, rows, width), bf),
            pltpu.VMEM((stretches, parts, rows // parts, width), bf),
            pltpu.VMEM(small, f32),
            pltpu.VMEM(small, f32),
            pltpu.VMEM((n,) + small, f32),
            pltpu.SemaphoreType.DMA((slots,)),
            pltpu.SemaphoreType.DMA((slots,)),
        ],
        compiler_params=pltpu.CompilerParams(
            collective_id=2, has_side_effects=True, vmem_limit_bytes=67043328
        ),
        name="blocks",
    )(fq, fk, fv, rates, aq, ak, av, wb, gain)


def local_blocks(fq, fk, fv, rates, aq, ak, av, fast_weights, gain):
    stretches, rows, _ = fq.shape
    heads = fast_weights.shape[2]
    shard = jnp.transpose(fast_weights, (1, 2, 0, 3)).astype(jnp.bfloat16)
    wb = lax.all_gather(shard, "aa", axis=0)
    rate = jnp.transpose(rates.reshape(stretches, rows, heads, 3), (0, 2, 3, 1))[..., None]
    mixed, weights, moment = run_blocks(fq, fk, fv, rate, aq, ak, av, wb, gain[None])
    back = (2, 0, 1, 3)
    return (mixed, jnp.transpose(weights, back), jnp.transpose(moment, back))


def pick(*args):
    stretches, rows, _ = args[0].shape
    r, _, _, depth = args[7].shape
    n, parts = lax.axis_size("aa"), lax.axis_size("ba")
    fits = r % 16 == 0 and n % 2 == 0 and n > 2 and depth % AD == 0 and stretches == 2
    fits = fits and 2 * rows == WINDOW and rows % (16 * parts) == 0
    return (local_blocks if fits else local)(*args)


def solution(mesh):
    token = P(None, "aa", "ba")
    hidden = P("aa", None, "ba", None)
    return jax.shard_map(
        pick,
        mesh=mesh,
        in_specs=(token,) * 7 + (hidden, P()),
        out_specs=(P(None, ("aa", "ba"), None), hidden, hidden),
        check_vma=False,
    )
```

```python
import functools
import math

import jax
import jax.numpy as jnp
from jax import lax
from jax.experimental import pallas as pl
from jax.experimental.pallas import tpu as pltpu
from jax.sharding import PartitionSpec as P

AD = 128
WINDOW = 512


BETA = 0.9
EPS = 1e-06


def shift(x, axis, by):
    length = lax.axis_size(axis)
    return lax.ppermute(x, axis, [(i, (i + by) % length) for i in range(length)])


def activation(x):
    sig = jax.nn.sigmoid(x)
    return (x * sig, sig * (1.0 + x * (1.0 - sig)))


def project(x, w):
    return jnp.einsum("nhd,hfd->nhf", x, w, preferred_element_type=jnp.float32)


def forward(w, query):
    rows, heads = query.shape[0], w.shape[1]
    q = query.reshape(rows, heads, -1)
    act_q, _ = activation(project(q, w[0]))
    hidden_q = (act_q * project(q, w[1])).astype(jnp.bfloat16)
    return jnp.einsum("nhf,hfd->nhd", hidden_q, w[2], preferred_element_type=jnp.float32).reshape(
        rows, -1
    )


def partial_grads(w, key, value, rate):
    rows, heads = key.shape[0], w.shape[1]
    k = key.reshape(rows, heads, -1)
    v = value.reshape(rows, heads, -1)
    gate_in = project(k, w[0])
    up_in = project(k, w[1])
    back_in = project(v, w[2])
    act, slope = activation(gate_in)
    gate_x = (rate[..., 0:1] * (-back_in * up_in * slope)).astype(jnp.bfloat16)
    up_x = (rate[..., 1:2] * (-back_in * act)).astype(jnp.bfloat16)
    down_x = (rate[..., 2:3] * -(act * up_in)).astype(jnp.bfloat16)

    def part(left, right):
        return jnp.einsum("nhf,nhd->hfd", left, right, preferred_element_type=jnp.float32)

    return jnp.stack([part(gate_x, k), part(up_x, k), part(down_x, v)]).astype(jnp.bfloat16)


def attend_kernel(rows, groups, q_ref, *refs):
    out_ref = refs[-1]
    stretch = pl.program_id(0)
    base = stretch * (rows * groups) + lax.axis_index("aa") * rows
    q = q_ref[0]
    scores = []
    blocks = (len(refs) - 1) // 2
    row = lax.broadcasted_iota(jnp.int32, (rows, rows), 0)
    col = lax.broadcasted_iota(jnp.int32, (rows, rows), 1)
    for back in range(blocks):
        s = lax.dot_general(
            q, refs[back][0], (((1,), (1,)), ((), ())), preferred_element_type=jnp.float32
        ) / math.sqrt(AD)
        gap = row - col + back * rows
        ok = (gap >= 0) & (gap < WINDOW) & (col >= back * rows - base)
        scores.append(jnp.where(ok, s, -1e30))
    top = functools.reduce(jnp.maximum, [jnp.max(s, -1, keepdims=True) for s in scores])
    total = 0.0
    acc = 0.0
    for back in range(blocks):
        p = jnp.exp(scores[back] - top)
        total = total + jnp.sum(p, -1, keepdims=True)
        acc = acc + jnp.dot(
            p.astype(jnp.bfloat16), refs[blocks + back][0], preferred_element_type=jnp.float32
        )
    out_ref[0] = acc / total


def attend(q, keys, values):
    stretches, rows, width = q.shape
    groups = lax.axis_size("aa")
    own = pl.BlockSpec((1, rows, AD), lambda s, h: (s, 0, h))
    index = lax.axis_index("aa")

    def moved(x, back):
        if not back:
            return x
        return jnp.where(index < back, jnp.concatenate([x[:1], x[:-1]], 0), x)

    keys = [moved(x, b) for b, x in enumerate(keys)]
    values = [moved(x, b) for b, x in enumerate(values)]
    return pl.pallas_call(
        functools.partial(attend_kernel, rows, groups),
        grid=(stretches, width // AD),
        in_specs=[own] * (1 + 2 * len(keys)),
        out_specs=own,
        out_shape=jax.ShapeDtypeStruct(q.shape, jnp.float32),
        cost_estimate=pl.CostEstimate(
            flops=4 * stretches * rows * rows * len(keys) * width,
            bytes_accessed=40 * q.size,
            transcendentals=stretches * rows * rows * len(keys) * width // AD,
        ),
        name="attend",
    )(q, *keys, *values)


def sum_kernel(n, x_ref, out_ref, land, send_sem, recv_sem):
    me = lax.axis_index("aa")
    barrier = pltpu.get_barrier_semaphore()
    for step in range(1, n):
        pl.semaphore_signal(
            barrier,
            inc=1,
            device_id={"aa": lax.rem(me + step, n)},
            device_id_type=pl.DeviceIdType.MESH,
        )
    pl.semaphore_wait(barrier, n - 1)
    copies = []
    for step in range(1, n):
        copy = pltpu.make_async_remote_copy(
            src_ref=x_ref,
            dst_ref=land.at[step],
            send_sem=send_sem.at[step],
            recv_sem=recv_sem.at[step],
            device_id={"aa": lax.rem(me + step, n)},
            device_id_type=pl.DeviceIdType.MESH,
        )
        copy.start()
        copies.append(copy)
    total = x_ref[...]
    for step in range(1, n):
        copies[step - 1].wait_recv()
        total = total + land[step]
    for copy in copies:
        copy.wait_send()
    out_ref[...] = total


def sum_over(x):
    n = lax.axis_size("aa")
    vmem = pl.BlockSpec(memory_space=pltpu.VMEM)
    return pl.pallas_call(
        functools.partial(sum_kernel, n),
        in_specs=[vmem],
        out_specs=vmem,
        out_shape=jax.ShapeDtypeStruct(x.shape, x.dtype),
        scratch_shapes=[
            pltpu.VMEM((n,) + x.shape, x.dtype),
            pltpu.SemaphoreType.DMA((n,)),
            pltpu.SemaphoreType.DMA((n,)),
        ],
        compiler_params=pltpu.CompilerParams(collective_id=1, has_side_effects=True),
        name="sum_over",
    )(x)


def tie(values, anchor):
    out = lax.optimization_barrier(tuple(values) + (anchor,))
    return out[:-1], out[-1]


def local(
    fast_query, fast_key, fast_value, rates, attn_query, attn_key, attn_value, fast_weights, gain
):
    stretches, rows, width = fast_query.shape
    local_rows = fast_weights.shape[0]
    heads = fast_weights.shape[2]
    rate = rates.reshape(stretches, rows, heads, 3)
    index = lax.axis_index("aa")
    groups = lax.axis_size("aa")
    first_row = index * local_rows

    shard = jnp.transpose(fast_weights, (1, 2, 0, 3))
    wb = lax.all_gather(shard.astype(jnp.bfloat16), "aa", axis=2, tiled=True)
    (attn_key, attn_value), wb = tie((attn_key, attn_value), wb)
    far = [shift(attn_key, "aa", 2), shift(attn_value, "aa", 2)]

    full = wb.astype(jnp.float32)
    target = jnp.sqrt(jnp.sum(full * full, 2, keepdims=True) + EPS)
    gp = partial_grads(wb, fast_key[0], fast_value[0], rate[0])
    grads = lax.psum(gp, "aa").astype(jnp.float32)

    (fq,), _ = tie((fast_query,), gp)
    out0 = forward(wb, fq[0])
    far, out0 = tie(far, out0)
    odd = index % 2 == 1
    swap = [(i, i ^ 1) for i in range(groups)]
    near = [
        lax.ppermute(jnp.where(odd, f, o), "aa", swap) for f, o in zip(far, (attn_key, attn_value))
    ]
    attention = attend(
        attn_query, [attn_key, near[0], far[0]], [attn_value, near[1], far[1]]
    )
    (attention,), grads = tie((attention,), grads)

    trial = full - grads
    updated = trial * (target / jnp.sqrt(jnp.sum(trial * trial, 2, keepdims=True) + EPS))
    ub = updated.astype(jnp.bfloat16)
    gp1 = partial_grads(ub, fast_key[1], fast_value[1], rate[1])
    grads1 = lax.psum_scatter(gp1, "aa", scatter_dimension=2, tiled=True).astype(jnp.float32)
    (fq1,), _ = tie((fast_query,), gp1)
    out1 = forward(ub, fq1[1])
    combined = (jnp.stack([out0, out1]) + attention).astype(jnp.bfloat16)

    moment = BETA * lax.dynamic_slice_in_dim(grads, first_row, local_rows, 2) + grads1
    own = lax.dynamic_slice_in_dim(updated, first_row, local_rows, 2)
    trial = own - moment
    squares = sum_over(jnp.sum(trial * trial, 2).reshape(-1, trial.shape[3]))
    squares = squares.reshape(trial.shape[:2] + (1, trial.shape[3]))
    weights = trial * (target / jnp.sqrt(squares + EPS))

    arrived = lax.all_to_all(combined, "ba", split_axis=1, concat_axis=2, tiled=True)
    values = arrived.astype(jnp.float32)
    scale = lax.rsqrt(jnp.mean(values * values, -1, keepdims=True) + EPS)
    mixed = (values * scale * gain).astype(jnp.bfloat16)
    back = (2, 0, 1, 3)
    return (mixed, jnp.transpose(weights, back), jnp.transpose(moment, back))


class Comm:
    def __init__(self, send, recv):
        self.send, self.recv, self.used = send, recv, 0

    def slots(self, count):
        first = self.used
        self.used += count
        return first

    def make(self, slot, src, dst, peer, lands=None):
        return pltpu.make_async_remote_copy(
            src_ref=src,
            dst_ref=dst,
            send_sem=self.send.at[slot],
            recv_sem=self.recv.at[slot if lands is None else lands],
            device_id=peer,
            device_id_type=pl.DeviceIdType.MESH,
        )


NT = (((1,), (1,)), ((), ()))
TN = (((0,), (0,)), ((), ()))
NN = (((1,), (0,)), ((), ()))


def block_kernel(
    n,
    parts,
    fq,
    fk,
    fv,
    rate,
    aq,
    ak,
    av,
    shard,
    gain,
    mixed,
    weights,
    moment,
    gp,
    pair,
    first_sums,
    second_sums,
    first_land,
    second_land,
    start,
    full,
    far,
    near,
    relay,
    acc,
    comb,
    land,
    target,
    sq,
    sqland,
    send,
    recv,
):
    me = lax.axis_index("aa")
    mine = lax.axis_index("ba")
    group, core = me // 2, lax.rem(me, 2)
    teams = n // 2
    heads, _, r, depth = shard.shape
    stretches, rows, width = fq.shape
    row_at, col_at = group // 2, lax.rem(group, 2)
    beside = row_at * 2 + 1 - col_at
    above = (1 - row_at) * 2 + col_at
    across = (1 - row_at) * 2 + 1 - col_at
    partner = {"aa": group * 2 + 1 - core}
    to_x = {"aa": beside * 2 + core}
    to_y = {"aa": above * 2 + core}
    comm = Comm(send, recv)
    bf, f32 = jnp.bfloat16, jnp.float32
    via_y, via_x = pl.ds(0, 2), pl.ds(2, 1)

    barrier = pltpu.get_barrier_semaphore()
    for step in range(1, n):
        pl.semaphore_signal(
            barrier,
            inc=1,
            device_id={"aa": lax.rem(me + step, n)},
            device_id_type=pl.DeviceIdType.MESH,
        )
    for step in range(1, parts):
        pl.semaphore_signal(
            barrier,
            inc=1,
            device_id={"ba": lax.rem(mine + step, parts)},
            device_id_type=pl.DeviceIdType.MESH,
        )
    pl.semaphore_wait(barrier, n + parts - 2)

    held = (ak, av)
    final = comm.slots(2 * stretches)
    relays = comm.slots(stretches)
    swaps = comm.slots(2 * stretches)

    def halo_copy(t, s, direct):
        slot = final + t * stretches + s
        if direct:
            return comm.make(slot, held[t].at[s], far.at[t, s], to_x)
        return comm.make(slot, held[t].at[s], relay.at[s], (to_x, to_y)[t], relays + s)

    def halo(s):
        for t in range(2):

            @pl.when(col_at == 0)
            def _():
                halo_copy(t, s, True).start()

            @pl.when(col_at == 1)
            def _():
                halo_copy(t, s, False).start()

    def halo_relay(s):
        halo_copy(0, s, False).wait_recv()

        @pl.when(col_at == 0)
        def _():
            comm.make(relays + s, relay.at[s], far.at[0, s], to_y, final + s).start()

        @pl.when(col_at == 1)
        def _():
            comm.make(
                relays + s, relay.at[s], far.at[1, s], to_x, final + stretches + s
            ).start()

    def halo_swap(s):
        copies = []
        for t in range(2):
            slot = swaps + t * stretches + s
            halo_copy(t, s, True).wait_recv()

            @pl.when(core == 0)
            def _():
                comm.make(slot, held[t].at[s], near.at[t, s], partner).start()

            @pl.when(core == 1)
            def _():
                comm.make(slot, far.at[t, s], near.at[t, s], partner).start()

            copies.append(comm.make(slot, held[t].at[s], near.at[t, s], partner))
        for copy in copies:
            copy.wait()

    def halo_sent(s):
        for t in range(2):
            halo_copy(t, s, True).wait_send()
        comm.make(relays + s, relay.at[s], far.at[0, s], to_y).wait_send()

    def gather_start(buf, h, src):
        first = comm.slots(9)
        own = buf.at[h, me]
        copies = [
            comm.make(first, src, own, to_x),
            comm.make(first + 1, src, own, to_y),
            comm.make(first + 4, src, own, partner),
        ]
        for copy in copies:
            copy.start()
        return first, copies

    def gather_relay(buf, h, state):
        first, copies = state
        for k, (block, peer, ms) in enumerate(((beside, to_y, via_y), (above, to_x, via_x))):
            copies[k].wait_recv()
            at = block * 2 + core
            piece = buf.at[h, at, ms]
            onward = comm.make(first + 2 + k, piece, piece, peer)
            onward.start()
            twin = comm.make(first + 5 + k, buf.at[h, at], buf.at[h, at], partner)
            twin.start()
            copies += [onward, twin]

    def gather_end(buf, h, state):
        first, copies = state
        at = across * 2 + core
        for k, ms in enumerate((via_y, via_x)):
            piece = buf.at[h, at, ms]
            comm.make(first + 2 + k, piece, piece, partner).wait_recv()
            twin = comm.make(first + 7 + k, piece, piece, partner)
            twin.start()
            copies.append(twin)
        copies[2].wait_recv()
        copies[4].wait_recv()
        copies[6].wait_recv()
        copies[7].wait_recv()
        copies[8].wait_recv()
        for copy in copies:
            copy.wait_send()

    def mm(a, b, dims):
        return lax.dot_general(a, b, dims, preferred_element_type=f32)

    def whole(ref, m, h):
        return ref[h, :, m].reshape(n * r, depth)

    def grads(ref, s, h):
        cols = pl.ds(h * depth, depth)
        k = fk[s, :, cols]
        v = fv[s, :, cols]
        gate_in = mm(k, whole(ref, 0, h), NT)
        up_in = mm(k, whole(ref, 1, h), NT)
        back_in = mm(v, whole(ref, 2, h), NT)
        act, slope = activation(gate_in)
        xs = (
            (rate[s, h, 0] * (-back_in * up_in * slope)).astype(bf),
            (rate[s, h, 1] * (-back_in * act)).astype(bf),
            (rate[s, h, 2] * -(act * up_in)).astype(bf),
        )
        for m in range(3):
            part = mm(xs[m], v if m == 2 else k, TN).astype(bf).reshape(teams, 2, r, depth)
            for c in range(2):
                gp[h, c, :, m] = part[:, c]

    def forward(ref, s):
        @pl.loop(0, heads)
        def _(h):
            cols = pl.ds(pl.multiple_of(h * depth, 128), depth)
            q = fq[s, :, cols]
            act, _ = activation(mm(q, whole(ref, 0, h), NT))
            hidden = (act * mm(q, whole(ref, 1, h), NT)).astype(bf)
            acc[s, :, cols] = mm(hidden, whole(ref, 2, h), NN)

    def attention(s):
        base = s * (rows * n) + me * rows
        places = [s] + [jnp.where(me < b, max(s - 1, 0), s) for b in (1, 2)]
        row = lax.broadcasted_iota(jnp.int32, (rows, rows), 0)
        col = lax.broadcasted_iota(jnp.int32, (rows, rows), 1)
        oks = []
        for back in range(3):
            gap = row - col + back * rows
            oks.append((gap >= 0) & (gap < WINDOW) & (col >= back * rows - base))

        @pl.loop(0, width // AD)
        def _(h):
            cols = pl.ds(pl.multiple_of(h * AD, AD), AD)
            keys = [ak[s, :, cols], near[0, places[1], :, cols], far[0, places[2], :, cols]]
            values = [av[s, :, cols], near[1, places[1], :, cols], far[1, places[2], :, cols]]
            q = aq[s, :, cols]
            scores = [
                jnp.where(ok, mm(q, k, NT) / math.sqrt(AD), -1e30) for ok, k in zip(oks, keys)
            ]
            top = functools.reduce(
                jnp.maximum, [jnp.max(x, -1, keepdims=True) for x in scores]
            )
            total, out = 0.0, 0.0
            for x, v in zip(scores, values):
                p = jnp.exp(x - top)
                total = total + jnp.sum(p, -1, keepdims=True)
                out = out + mm(p.astype(bf), v, NN)
            comb[s, :, cols] = (acc[s, :, cols] + out / total).astype(bf)

    def pair_send(phase, h):
        slot = comm.slots(1)
        copy = comm.make(slot, gp.at[h, 1 - core], pair.at[phase, h], partner)
        copy.start()
        return copy

    def both(phase, h, g, m):
        return gp[h, core, g, m].astype(f32) + pair[phase, h, g, m].astype(f32)

    def reduce_first(phase, h, copy):
        copy.wait()
        for k, g in enumerate((above, across)):
            for m in range(2):
                first_sums[h, k, m] = both(phase, h, g, m).astype(bf)
        for k, g in enumerate((beside, across)):
            first_sums[h, 2 + k, 0] = both(phase, h, g, 2).astype(bf)
        slot = comm.slots(3)
        copies = [
            comm.make(
                slot,
                first_sums.at[h, pl.ds(0, 2)],
                first_land.at[phase, h, pl.ds(0, 2)],
                to_y,
            )
        ]
        for k in range(2, 4):
            copies.append(
                comm.make(
                    slot + k - 1,
                    first_sums.at[h, k, pl.ds(0, 1)],
                    first_land.at[phase, h, k, pl.ds(0, 1)],
                    to_x,
                )
            )
        for copy in copies:
            copy.start()
        return copies

    def reduce_second(phase, h, copies):
        for copy in copies:
            copy.wait()
        for m in range(2):
            second_sums[h, m] = (
                both(phase, h, beside, m) + first_land[phase, h, 1, m].astype(f32)
            ).astype(bf)
        second_sums[h, 2] = (
            both(phase, h, above, 2) + first_land[phase, h, 3, 0].astype(f32)
        ).astype(bf)
        slot = comm.slots(2)
        out = []
        for k, (peer, ms) in enumerate(((to_x, via_y), (to_y, via_x))):
            copy = comm.make(
                slot + k, second_sums.at[h, ms], second_land.at[phase, h, ms], peer
            )
            copy.start()
            out.append(copy)
        return out

    def total_of(phase, h, m):
        got = first_land[phase, h, 0, m] if m < 2 else first_land[phase, h, 2, 0]
        return (
            both(phase, h, group, m) + got.astype(f32) + second_land[phase, h, m].astype(f32)
        )

    def exchange(s):
        first = comm.slots(parts)
        chunk = rows // parts
        copies = []
        for step in range(1, parts):
            z = lax.rem(mine + step, parts)
            take = pl.ds(pl.multiple_of(z * chunk, chunk), chunk)
            copy = comm.make(first + step, comb.at[s, take], land.at[s, step], {"ba": z})
            copy.start()
            copies.append(copy)
        return copies

    def finish(s, copies):
        chunk = rows // parts
        take = pl.ds(pl.multiple_of(mine * chunk, chunk), chunk)
        land[s, 0] = comb[s, take]
        for copy in copies:
            copy.wait()
        squares = 0.0
        for step in range(parts):
            x = land[s, step].astype(f32)
            squares = squares + jnp.sum(x * x, -1, keepdims=True)
        scale = lax.rsqrt(squares / (parts * width) + EPS)
        for step in range(parts):
            z = lax.rem(mine + parts - step, parts)
            cols = pl.ds(pl.multiple_of(z * width, 128), width)
            x = land[s, step].astype(f32)
            mixed[s, :, cols] = (x * scale * gain[:, cols]).astype(bf)

    def renorm(h):
        for m in range(3):
            before, after = 0.0, 0.0
            for j in range(n):
                w = start[h, j, m].astype(f32)
                t = w - full[h, j, m].astype(f32)
                before = before + jnp.sum(w * w, 0, keepdims=True)
                after = after + jnp.sum(t * t, 0, keepdims=True)
            goal = jnp.sqrt(before + EPS)
            target[h, m] = goal
            ratio = goal / jnp.sqrt(after + EPS)
            past = full[h, me, m].astype(f32)
            moment[h, m] = past
            weights[h, m] = (start[h, me, m].astype(f32) - past) * ratio
            for j in range(n):
                w = start[h, j, m].astype(f32)
                t = w - full[h, j, m].astype(f32)
                full[h, j, m] = (t * ratio).astype(bf)

    each = range(heads)
    states = []
    for h in each:
        start[h, me] = shard[h]
        states.append(gather_start(start, h, shard.at[h]))
    for h in each:
        gather_relay(start, h, states[h])
    halo(0)
    pairs = []
    for h in each:
        gather_end(start, h, states[h])
        grads(start, 0, h)
        pairs.append(pair_send(0, h))
    firsts = [reduce_first(0, h, pairs[h]) for h in each]
    forward(start, 0)
    halo_relay(0)
    seconds = [reduce_second(0, h, firsts[h]) for h in each]
    halo_swap(0)
    attention(0)
    mixing0 = exchange(0)
    states = []
    for h in each:
        for copy in seconds[h]:
            copy.wait()
        for m in range(3):
            full[h, me, m] = total_of(0, h, m).astype(bf)
        states.append(gather_start(full, h, full.at[h, me]))
    for h in each:
        gather_relay(full, h, states[h])
    halo(1)
    pairs = []
    for h in each:
        gather_end(full, h, states[h])
        renorm(h)
        grads(full, 1, h)
        pairs.append(pair_send(1, h))
    firsts = [reduce_first(1, h, pairs[h]) for h in each]
    forward(full, 1)
    halo_relay(1)
    seconds = [reduce_second(1, h, firsts[h]) for h in each]
    finish(0, mixing0)
    halo_swap(1)
    attention(1)
    mixing1 = exchange(1)
    for h in each:
        for copy in seconds[h]:
            copy.wait()
        for m in range(3):
            momentum = BETA * moment[h, m] + total_of(1, h, m)
            moment[h, m] = momentum
            trial = weights[h, m] - momentum
            weights[h, m] = trial
            sq[h, m] = jnp.sum(trial * trial, 0, keepdims=True)

    first = comm.slots(n)
    copies = []
    for step in range(1, n):
        copy = comm.make(
            first + step, sq, sqland.at[step], {"aa": lax.rem(me + step, n)}
        )
        copy.start()
        copies.append(copy)
    finish(1, mixing1)
    for copy in copies:
        copy.wait()
    for h in each:
        for m in range(3):
            squares = sq[h, m]
            for step in range(1, n):
                squares = squares + sqland[step, h, m]
            weights[h, m] = weights[h, m] * (target[h, m] / jnp.sqrt(squares + EPS))
    for s in range(stretches):
        halo_sent(s)


def run_blocks(fq, fk, fv, rates, aq, ak, av, shard, gain):
    n, parts = lax.axis_size("aa"), lax.axis_size("ba")
    stretches, rows, width = fq.shape
    heads, _, r, depth = shard.shape
    teams = n // 2
    vmem = pl.BlockSpec(memory_space=pltpu.VMEM)
    piece = (3, r, depth)
    small = (heads, 3, 1, depth)
    bf, f32 = jnp.bfloat16, jnp.float32
    slots = 5 * stretches + heads * 2 * (9 + 1 + 3 + 2) + 2 * parts + n
    return pl.pallas_call(
        functools.partial(block_kernel, n, parts),
        in_specs=[vmem] * 9,
        out_specs=(vmem,) * 3,
        out_shape=(
            jax.ShapeDtypeStruct((stretches, rows // parts, width * parts), bf),
            jax.ShapeDtypeStruct((heads,) + piece, f32),
            jax.ShapeDtypeStruct((heads,) + piece, f32),
        ),
        scratch_shapes=[
            pltpu.VMEM((heads, 2, teams) + piece, bf),
            pltpu.VMEM((2, heads, teams) + piece, bf),
            pltpu.VMEM((heads, 4, 2, r, depth), bf),
            pltpu.VMEM((heads,) + piece, bf),
            pltpu.VMEM((2, heads, 4, 2, r, depth), bf),
            pltpu.VMEM((2, heads) + piece, bf),
            pltpu.VMEM((heads, n) + piece, bf),
            pltpu.VMEM((heads, n) + piece, bf),
            pltpu.VMEM((2, stretches, rows, width), bf),
            pltpu.VMEM((2, stretches, rows, width), bf),
            pltpu.VMEM((stretches, rows, width), bf),
            pltpu.VMEM((stretches, rows, width), f32),
            pltpu.VMEM((stretches, rows, width), bf),
            pltpu.VMEM((stretches, parts, rows // parts, width), bf),
            pltpu.VMEM(small, f32),
            pltpu.VMEM(small, f32),
            pltpu.VMEM((n,) + small, f32),
            pltpu.SemaphoreType.DMA((slots,)),
            pltpu.SemaphoreType.DMA((slots,)),
        ],
        compiler_params=pltpu.CompilerParams(
            collective_id=2, has_side_effects=True, vmem_limit_bytes=67043328
        ),
        name="blocks",
    )(fq, fk, fv, rates, aq, ak, av, shard, gain)


def local_blocks(fq, fk, fv, rates, aq, ak, av, fast_weights, gain):
    stretches, rows, _ = fq.shape
    heads = fast_weights.shape[2]
    shard = jnp.transpose(fast_weights.astype(jnp.bfloat16), (2, 1, 0, 3))
    rate = jnp.transpose(rates.reshape(stretches, rows, heads, 3), (0, 2, 3, 1))[..., None]
    mixed, weights, moment = run_blocks(fq, fk, fv, rate, aq, ak, av, shard, gain[None])
    back = (2, 1, 0, 3)
    return (mixed, jnp.transpose(weights, back), jnp.transpose(moment, back))


def pick(*args):
    stretches, rows, _ = args[0].shape
    r, _, _, depth = args[7].shape
    n, parts = lax.axis_size("aa"), lax.axis_size("ba")
    fits = r % 16 == 0 and n == 8 and depth % AD == 0 and stretches == 2
    fits = fits and 2 * rows == WINDOW and rows % (16 * parts) == 0
    return (local_blocks if fits else local)(*args)


def solution(mesh):
    token = P(None, "aa", "ba")
    hidden = P("aa", None, "ba", None)
    return jax.shard_map(
        pick,
        mesh=mesh,
        in_specs=(token,) * 7 + (hidden, P()),
        out_specs=(P(None, ("aa", "ba"), None), hidden, hidden),
        check_vma=False,
    )
```

```python
import functools
import math

import jax
import jax.numpy as jnp
from jax import lax
from jax.experimental import pallas as pl
from jax.experimental.pallas import tpu as pltpu
from jax.sharding import PartitionSpec as P

AD = 128
WINDOW = 512


BETA = 0.9
EPS = 1e-06


def shift(x, axis, by):
    length = lax.axis_size(axis)
    return lax.ppermute(x, axis, [(i, (i + by) % length) for i in range(length)])


def activation(x):
    sig = jax.nn.sigmoid(x)
    return (x * sig, sig * (1.0 + x * (1.0 - sig)))


def project(x, w):
    return jnp.einsum("nhd,hfd->nhf", x, w, preferred_element_type=jnp.float32)


def forward(w, query):
    rows, heads = query.shape[0], w.shape[1]
    q = query.reshape(rows, heads, -1)
    act_q, _ = activation(project(q, w[0]))
    hidden_q = (act_q * project(q, w[1])).astype(jnp.bfloat16)
    return jnp.einsum("nhf,hfd->nhd", hidden_q, w[2], preferred_element_type=jnp.float32).reshape(
        rows, -1
    )


def partial_grads(w, key, value, rate):
    rows, heads = key.shape[0], w.shape[1]
    k = key.reshape(rows, heads, -1)
    v = value.reshape(rows, heads, -1)
    gate_in = project(k, w[0])
    up_in = project(k, w[1])
    back_in = project(v, w[2])
    act, slope = activation(gate_in)
    gate_x = (rate[..., 0:1] * (-back_in * up_in * slope)).astype(jnp.bfloat16)
    up_x = (rate[..., 1:2] * (-back_in * act)).astype(jnp.bfloat16)
    down_x = (rate[..., 2:3] * -(act * up_in)).astype(jnp.bfloat16)

    def part(left, right):
        return jnp.einsum("nhf,nhd->hfd", left, right, preferred_element_type=jnp.float32)

    return jnp.stack([part(gate_x, k), part(up_x, k), part(down_x, v)]).astype(jnp.bfloat16)


def attend_kernel(rows, groups, q_ref, *refs):
    out_ref = refs[-1]
    stretch = pl.program_id(0)
    base = stretch * (rows * groups) + lax.axis_index("aa") * rows
    q = q_ref[0]
    scores = []
    blocks = (len(refs) - 1) // 2
    row = lax.broadcasted_iota(jnp.int32, (rows, rows), 0)
    col = lax.broadcasted_iota(jnp.int32, (rows, rows), 1)
    for back in range(blocks):
        s = lax.dot_general(
            q, refs[back][0], (((1,), (1,)), ((), ())), preferred_element_type=jnp.float32
        ) / math.sqrt(AD)
        gap = row - col + back * rows
        ok = (gap >= 0) & (gap < WINDOW) & (col >= back * rows - base)
        scores.append(jnp.where(ok, s, -1e30))
    top = functools.reduce(jnp.maximum, [jnp.max(s, -1, keepdims=True) for s in scores])
    total = 0.0
    acc = 0.0
    for back in range(blocks):
        p = jnp.exp(scores[back] - top)
        total = total + jnp.sum(p, -1, keepdims=True)
        acc = acc + jnp.dot(
            p.astype(jnp.bfloat16), refs[blocks + back][0], preferred_element_type=jnp.float32
        )
    out_ref[0] = acc / total


def attend(q, keys, values):
    stretches, rows, width = q.shape
    groups = lax.axis_size("aa")
    own = pl.BlockSpec((1, rows, AD), lambda s, h: (s, 0, h))
    index = lax.axis_index("aa")

    def moved(x, back):
        if not back:
            return x
        return jnp.where(index < back, jnp.concatenate([x[:1], x[:-1]], 0), x)

    keys = [moved(x, b) for b, x in enumerate(keys)]
    values = [moved(x, b) for b, x in enumerate(values)]
    return pl.pallas_call(
        functools.partial(attend_kernel, rows, groups),
        grid=(stretches, width // AD),
        in_specs=[own] * (1 + 2 * len(keys)),
        out_specs=own,
        out_shape=jax.ShapeDtypeStruct(q.shape, jnp.float32),
        cost_estimate=pl.CostEstimate(
            flops=4 * stretches * rows * rows * len(keys) * width,
            bytes_accessed=40 * q.size,
            transcendentals=stretches * rows * rows * len(keys) * width // AD,
        ),
        name="attend",
    )(q, *keys, *values)


def sum_kernel(n, x_ref, out_ref, land, send_sem, recv_sem):
    me = lax.axis_index("aa")
    barrier = pltpu.get_barrier_semaphore()
    for step in range(1, n):
        pl.semaphore_signal(
            barrier,
            inc=1,
            device_id={"aa": lax.rem(me + step, n)},
            device_id_type=pl.DeviceIdType.MESH,
        )
    pl.semaphore_wait(barrier, n - 1)
    copies = []
    for step in range(1, n):
        copy = pltpu.make_async_remote_copy(
            src_ref=x_ref,
            dst_ref=land.at[step],
            send_sem=send_sem.at[step],
            recv_sem=recv_sem.at[step],
            device_id={"aa": lax.rem(me + step, n)},
            device_id_type=pl.DeviceIdType.MESH,
        )
        copy.start()
        copies.append(copy)
    total = x_ref[...]
    for step in range(1, n):
        copies[step - 1].wait_recv()
        total = total + land[step]
    for copy in copies:
        copy.wait_send()
    out_ref[...] = total


def sum_over(x):
    n = lax.axis_size("aa")
    vmem = pl.BlockSpec(memory_space=pltpu.VMEM)
    return pl.pallas_call(
        functools.partial(sum_kernel, n),
        in_specs=[vmem],
        out_specs=vmem,
        out_shape=jax.ShapeDtypeStruct(x.shape, x.dtype),
        scratch_shapes=[
            pltpu.VMEM((n,) + x.shape, x.dtype),
            pltpu.SemaphoreType.DMA((n,)),
            pltpu.SemaphoreType.DMA((n,)),
        ],
        compiler_params=pltpu.CompilerParams(collective_id=1, has_side_effects=True),
        name="sum_over",
    )(x)


def tie(values, anchor):
    out = lax.optimization_barrier(tuple(values) + (anchor,))
    return out[:-1], out[-1]


def local(
    fast_query, fast_key, fast_value, rates, attn_query, attn_key, attn_value, fast_weights, gain
):
    stretches, rows, width = fast_query.shape
    local_rows = fast_weights.shape[0]
    heads = fast_weights.shape[2]
    rate = rates.reshape(stretches, rows, heads, 3)
    index = lax.axis_index("aa")
    groups = lax.axis_size("aa")
    first_row = index * local_rows

    shard = jnp.transpose(fast_weights, (1, 2, 0, 3))
    wb = lax.all_gather(shard.astype(jnp.bfloat16), "aa", axis=2, tiled=True)
    (attn_key, attn_value), wb = tie((attn_key, attn_value), wb)
    far = [shift(attn_key, "aa", 2), shift(attn_value, "aa", 2)]

    full = wb.astype(jnp.float32)
    target = jnp.sqrt(jnp.sum(full * full, 2, keepdims=True) + EPS)
    gp = partial_grads(wb, fast_key[0], fast_value[0], rate[0])
    grads = lax.psum(gp, "aa").astype(jnp.float32)

    (fq,), _ = tie((fast_query,), gp)
    out0 = forward(wb, fq[0])
    far, out0 = tie(far, out0)
    odd = index % 2 == 1
    swap = [(i, i ^ 1) for i in range(groups)]
    near = [
        lax.ppermute(jnp.where(odd, f, o), "aa", swap) for f, o in zip(far, (attn_key, attn_value))
    ]
    attention = attend(
        attn_query, [attn_key, near[0], far[0]], [attn_value, near[1], far[1]]
    )
    (attention,), grads = tie((attention,), grads)

    trial = full - grads
    updated = trial * (target / jnp.sqrt(jnp.sum(trial * trial, 2, keepdims=True) + EPS))
    ub = updated.astype(jnp.bfloat16)
    gp1 = partial_grads(ub, fast_key[1], fast_value[1], rate[1])
    grads1 = lax.psum_scatter(gp1, "aa", scatter_dimension=2, tiled=True).astype(jnp.float32)
    (fq1,), _ = tie((fast_query,), gp1)
    out1 = forward(ub, fq1[1])
    combined = (jnp.stack([out0, out1]) + attention).astype(jnp.bfloat16)

    moment = BETA * lax.dynamic_slice_in_dim(grads, first_row, local_rows, 2) + grads1
    own = lax.dynamic_slice_in_dim(updated, first_row, local_rows, 2)
    trial = own - moment
    squares = sum_over(jnp.sum(trial * trial, 2).reshape(-1, trial.shape[3]))
    squares = squares.reshape(trial.shape[:2] + (1, trial.shape[3]))
    weights = trial * (target / jnp.sqrt(squares + EPS))

    arrived = lax.all_to_all(combined, "ba", split_axis=1, concat_axis=2, tiled=True)
    values = arrived.astype(jnp.float32)
    scale = lax.rsqrt(jnp.mean(values * values, -1, keepdims=True) + EPS)
    mixed = (values * scale * gain).astype(jnp.bfloat16)
    back = (2, 0, 1, 3)
    return (mixed, jnp.transpose(weights, back), jnp.transpose(moment, back))


class Comm:
    def __init__(self, send, recv):
        self.send, self.recv, self.used = send, recv, 0

    def slots(self, count):
        first = self.used
        self.used += count
        return first

    def make(self, slot, src, dst, peer, lands=None):
        return pltpu.make_async_remote_copy(
            src_ref=src,
            dst_ref=dst,
            send_sem=self.send.at[slot],
            recv_sem=self.recv.at[slot if lands is None else lands],
            device_id=peer,
            device_id_type=pl.DeviceIdType.MESH,
        )


NT = (((1,), (1,)), ((), ()))
TN = (((0,), (0,)), ((), ()))
NN = (((1,), (0,)), ((), ()))


def block_kernel(
    n,
    parts,
    fq,
    fk,
    fv,
    rate,
    aq,
    ak,
    av,
    shard,
    gain,
    mixed,
    weights,
    moment,
    gp,
    pair,
    first_sums,
    second_sums,
    first_land,
    second_land,
    start,
    full,
    far,
    near,
    relay,
    acc,
    comb,
    land,
    target,
    sq,
    sqland,
    send,
    recv,
):
    me = lax.axis_index("aa")
    mine = lax.axis_index("ba")
    group, core = me // 2, lax.rem(me, 2)
    teams = n // 2
    heads, _, r, depth = shard.shape
    stretches, rows, width = fq.shape
    row_at, col_at = group // 2, lax.rem(group, 2)
    beside = row_at * 2 + 1 - col_at
    above = (1 - row_at) * 2 + col_at
    across = (1 - row_at) * 2 + 1 - col_at
    partner = {"aa": group * 2 + 1 - core}
    to_x = {"aa": beside * 2 + core}
    to_y = {"aa": above * 2 + core}
    comm = Comm(send, recv)
    bf, f32 = jnp.bfloat16, jnp.float32
    via_y, via_x = pl.ds(0, 2), pl.ds(2, 1)

    barrier = pltpu.get_barrier_semaphore()
    for step in range(1, n):
        pl.semaphore_signal(
            barrier,
            inc=1,
            device_id={"aa": lax.rem(me + step, n)},
            device_id_type=pl.DeviceIdType.MESH,
        )
    for step in range(1, parts):
        pl.semaphore_signal(
            barrier,
            inc=1,
            device_id={"ba": lax.rem(mine + step, parts)},
            device_id_type=pl.DeviceIdType.MESH,
        )
    pl.semaphore_wait(barrier, n + parts - 2)

    held = (ak, av)
    final = comm.slots(2 * stretches)
    relays = comm.slots(stretches)
    swaps = comm.slots(2 * stretches)

    def halo_copy(t, s, direct):
        slot = final + t * stretches + s
        if direct:
            return comm.make(slot, held[t].at[s], far.at[t, s], to_x)
        return comm.make(slot, held[t].at[s], relay.at[s], (to_x, to_y)[t], relays + s)

    def halo(s):
        for t in range(2):

            @pl.when(col_at == 0)
            def _():
                halo_copy(t, s, True).start()

            @pl.when(col_at == 1)
            def _():
                halo_copy(t, s, False).start()

    def halo_relay(s):
        halo_copy(0, s, False).wait_recv()

        @pl.when(col_at == 0)
        def _():
            comm.make(relays + s, relay.at[s], far.at[0, s], to_y, final + s).start()

        @pl.when(col_at == 1)
        def _():
            comm.make(
                relays + s, relay.at[s], far.at[1, s], to_x, final + stretches + s
            ).start()

    def halo_swap(s):
        copies = []
        for t in range(2):
            slot = swaps + t * stretches + s
            halo_copy(t, s, True).wait_recv()

            @pl.when(core == 0)
            def _():
                comm.make(slot, held[t].at[s], near.at[t, s], partner).start()

            @pl.when(core == 1)
            def _():
                comm.make(slot, far.at[t, s], near.at[t, s], partner).start()

            copies.append(comm.make(slot, held[t].at[s], near.at[t, s], partner))
        return copies

    def halo_sent(s):
        for t in range(2):
            halo_copy(t, s, True).wait_send()
        comm.make(relays + s, relay.at[s], far.at[0, s], to_y).wait_send()

    def gather_start(buf, h, src):
        first = comm.slots(9)
        own = buf.at[h, me]
        copies = [
            comm.make(first, src, own, to_x),
            comm.make(first + 1, src, own, to_y),
            comm.make(first + 4, src, own, partner),
        ]
        for copy in copies:
            copy.start()
        return first, copies

    def gather_relay(buf, h, state):
        first, copies = state
        for k, (block, peer, ms) in enumerate(((beside, to_y, via_y), (above, to_x, via_x))):
            copies[k].wait_recv()
            at = block * 2 + core
            piece = buf.at[h, at, ms]
            onward = comm.make(first + 2 + k, piece, piece, peer)
            onward.start()
            twin = comm.make(first + 5 + k, buf.at[h, at], buf.at[h, at], partner)
            twin.start()
            copies += [onward, twin]

    def gather_end(buf, h, state):
        first, copies = state
        at = across * 2 + core
        for k, ms in enumerate((via_y, via_x)):
            piece = buf.at[h, at, ms]
            comm.make(first + 2 + k, piece, piece, partner).wait_recv()
            twin = comm.make(first + 7 + k, piece, piece, partner)
            twin.start()
            copies.append(twin)
        copies[2].wait_recv()
        copies[4].wait_recv()
        copies[6].wait_recv()
        copies[7].wait_recv()
        copies[8].wait_recv()
        for copy in copies:
            copy.wait_send()

    def mm(a, b, dims):
        return lax.dot_general(a, b, dims, preferred_element_type=f32)

    def whole(ref, m, h):
        return ref[h, :, m].reshape(n * r, depth)

    def grads(ref, s, h):
        cols = pl.ds(h * depth, depth)
        k = fk[s, :, cols]
        v = fv[s, :, cols]
        gate_in = mm(k, whole(ref, 0, h), NT)
        up_in = mm(k, whole(ref, 1, h), NT)
        back_in = mm(v, whole(ref, 2, h), NT)
        act, slope = activation(gate_in)
        xs = (
            (rate[s, h, 0] * (-back_in * up_in * slope)).astype(bf),
            (rate[s, h, 1] * (-back_in * act)).astype(bf),
            (rate[s, h, 2] * -(act * up_in)).astype(bf),
        )
        for m in range(3):
            part = mm(xs[m], v if m == 2 else k, TN).astype(bf).reshape(teams, 2, r, depth)
            for c in range(2):
                gp[h, c, :, m] = part[:, c]

    def forward(ref, s):
        @pl.loop(0, heads)
        def _(h):
            cols = pl.ds(pl.multiple_of(h * depth, 128), depth)
            q = fq[s, :, cols]
            act, _ = activation(mm(q, whole(ref, 0, h), NT))
            hidden = (act * mm(q, whole(ref, 1, h), NT)).astype(bf)
            acc[s, :, cols] = mm(hidden, whole(ref, 2, h), NN)

    def attention(s):
        base = s * (rows * n) + me * rows
        places = [s] + [jnp.where(me < b, max(s - 1, 0), s) for b in (1, 2)]
        row = lax.broadcasted_iota(jnp.int32, (rows, rows), 0)
        col = lax.broadcasted_iota(jnp.int32, (rows, rows), 1)
        oks = []
        for back in range(3):
            gap = row - col + back * rows
            oks.append((gap >= 0) & (gap < WINDOW) & (col >= back * rows - base))

        @pl.loop(0, width // AD)
        def _(h):
            cols = pl.ds(pl.multiple_of(h * AD, AD), AD)
            keys = [ak[s, :, cols], near[0, places[1], :, cols], far[0, places[2], :, cols]]
            values = [av[s, :, cols], near[1, places[1], :, cols], far[1, places[2], :, cols]]
            q = aq[s, :, cols]
            scores = [
                jnp.where(ok, mm(q, k, NT) / math.sqrt(AD), -1e30) for ok, k in zip(oks, keys)
            ]
            top = functools.reduce(
                jnp.maximum, [jnp.max(x, -1, keepdims=True) for x in scores]
            )
            total, out = 0.0, 0.0
            for x, v in zip(scores, values):
                p = jnp.exp(x - top)
                total = total + jnp.sum(p, -1, keepdims=True)
                out = out + mm(p.astype(bf), v, NN)
            comb[s, :, cols] = (acc[s, :, cols] + out / total).astype(bf)

    def pair_send(phase, h):
        slot = comm.slots(1)
        copy = comm.make(slot, gp.at[h, 1 - core], pair.at[phase, h], partner)
        copy.start()
        return copy

    def both(phase, h, g, m):
        return gp[h, core, g, m].astype(f32) + pair[phase, h, g, m].astype(f32)

    def reduce_first(phase, h, copy):
        copy.wait()
        for k, g in enumerate((above, across)):
            for m in range(2):
                first_sums[h, k, m] = both(phase, h, g, m).astype(bf)
        for k, g in enumerate((beside, across)):
            first_sums[h, 2 + k, 0] = both(phase, h, g, 2).astype(bf)
        slot = comm.slots(3)
        copies = [
            comm.make(
                slot,
                first_sums.at[h, pl.ds(0, 2)],
                first_land.at[phase, h, pl.ds(0, 2)],
                to_y,
            )
        ]
        for k in range(2, 4):
            copies.append(
                comm.make(
                    slot + k - 1,
                    first_sums.at[h, k, pl.ds(0, 1)],
                    first_land.at[phase, h, k, pl.ds(0, 1)],
                    to_x,
                )
            )
        for copy in copies:
            copy.start()
        return copies

    def reduce_second(phase, h, copies):
        for copy in copies:
            copy.wait()
        for m in range(2):
            second_sums[h, m] = (
                both(phase, h, beside, m) + first_land[phase, h, 1, m].astype(f32)
            ).astype(bf)
        second_sums[h, 2] = (
            both(phase, h, above, 2) + first_land[phase, h, 3, 0].astype(f32)
        ).astype(bf)
        slot = comm.slots(2)
        out = []
        for k, (peer, ms) in enumerate(((to_x, via_y), (to_y, via_x))):
            copy = comm.make(
                slot + k, second_sums.at[h, ms], second_land.at[phase, h, ms], peer
            )
            copy.start()
            out.append(copy)
        return out

    def total_of(phase, h, m):
        got = first_land[phase, h, 0, m] if m < 2 else first_land[phase, h, 2, 0]
        return (
            both(phase, h, group, m) + got.astype(f32) + second_land[phase, h, m].astype(f32)
        )

    def exchange(s):
        first = comm.slots(parts)
        chunk = rows // parts
        copies = []
        for step in range(1, parts):
            z = lax.rem(mine + step, parts)
            take = pl.ds(pl.multiple_of(z * chunk, chunk), chunk)
            copy = comm.make(first + step, comb.at[s, take], land.at[s, step], {"ba": z})
            copy.start()
            copies.append(copy)
        return copies

    def finish(s, copies):
        chunk = rows // parts
        take = pl.ds(pl.multiple_of(mine * chunk, chunk), chunk)
        land[s, 0] = comb[s, take]
        for copy in copies:
            copy.wait()
        squares = 0.0
        for step in range(parts):
            x = land[s, step].astype(f32)
            squares = squares + jnp.sum(x * x, -1, keepdims=True)
        scale = lax.rsqrt(squares / (parts * width) + EPS)
        for step in range(parts):
            z = lax.rem(mine + parts - step, parts)
            cols = pl.ds(pl.multiple_of(z * width, 128), width)
            x = land[s, step].astype(f32)
            mixed[s, :, cols] = (x * scale * gain[:, cols]).astype(bf)

    def renorm(h):
        for m in range(3):
            before, after = 0.0, 0.0
            for j in range(n):
                w = start[h, j, m].astype(f32)
                t = w - full[h, j, m].astype(f32)
                before = before + jnp.sum(w * w, 0, keepdims=True)
                after = after + jnp.sum(t * t, 0, keepdims=True)
            goal = jnp.sqrt(before + EPS)
            target[h, m] = goal
            ratio = goal / jnp.sqrt(after + EPS)
            past = full[h, me, m].astype(f32)
            moment[h, m] = past
            weights[h, m] = (start[h, me, m].astype(f32) - past) * ratio
            for j in range(n):
                w = start[h, j, m].astype(f32)
                t = w - full[h, j, m].astype(f32)
                full[h, j, m] = (t * ratio).astype(bf)

    each = range(heads)
    states = []
    for h in each:
        start[h, me] = shard[h]
        states.append(gather_start(start, h, shard.at[h]))
    for h in each:
        gather_relay(start, h, states[h])
    halo(0)
    pairs = []
    for h in each:
        gather_end(start, h, states[h])
        grads(start, 0, h)
        pairs.append(pair_send(0, h))
    firsts = [reduce_first(0, h, pairs[h]) for h in each]
    forward(start, 0)
    seconds = [reduce_second(0, h, firsts[h]) for h in each]
    halo_relay(0)
    states = []
    for h in each:
        for copy in seconds[h]:
            copy.wait()
        for m in range(3):
            full[h, me, m] = total_of(0, h, m).astype(bf)
        states.append(gather_start(full, h, full.at[h, me]))
    for h in each:
        gather_relay(full, h, states[h])
    halo(1)
    moves = halo_swap(0)
    pairs = []
    for h in each:
        gather_end(full, h, states[h])
        renorm(h)
        grads(full, 1, h)
        pairs.append(pair_send(1, h))
    firsts = [reduce_first(1, h, pairs[h]) for h in each]
    forward(full, 1)
    for copy in moves:
        copy.wait()
    attention(0)
    mixing0 = exchange(0)
    halo_relay(1)
    seconds = [reduce_second(1, h, firsts[h]) for h in each]
    moves = halo_swap(1)
    for copy in moves:
        copy.wait()
    attention(1)
    mixing1 = exchange(1)
    finish(0, mixing0)
    for h in each:
        for copy in seconds[h]:
            copy.wait()
        for m in range(3):
            momentum = BETA * moment[h, m] + total_of(1, h, m)
            moment[h, m] = momentum
            trial = weights[h, m] - momentum
            weights[h, m] = trial
            sq[h, m] = jnp.sum(trial * trial, 0, keepdims=True)

    first = comm.slots(n)
    copies = []
    for step in range(1, n):
        copy = comm.make(
            first + step, sq, sqland.at[step], {"aa": lax.rem(me + step, n)}
        )
        copy.start()
        copies.append(copy)
    finish(1, mixing1)
    for copy in copies:
        copy.wait()
    for h in each:
        for m in range(3):
            squares = sq[h, m]
            for step in range(1, n):
                squares = squares + sqland[step, h, m]
            weights[h, m] = weights[h, m] * (target[h, m] / jnp.sqrt(squares + EPS))
    for s in range(stretches):
        halo_sent(s)


def run_blocks(fq, fk, fv, rates, aq, ak, av, shard, gain):
    n, parts = lax.axis_size("aa"), lax.axis_size("ba")
    stretches, rows, width = fq.shape
    heads, _, r, depth = shard.shape
    teams = n // 2
    vmem = pl.BlockSpec(memory_space=pltpu.VMEM)
    piece = (3, r, depth)
    small = (heads, 3, 1, depth)
    bf, f32 = jnp.bfloat16, jnp.float32
    slots = 5 * stretches + heads * 2 * (9 + 1 + 3 + 2) + 2 * parts + n
    return pl.pallas_call(
        functools.partial(block_kernel, n, parts),
        in_specs=[vmem] * 9,
        out_specs=(vmem,) * 3,
        out_shape=(
            jax.ShapeDtypeStruct((stretches, rows // parts, width * parts), bf),
            jax.ShapeDtypeStruct((heads,) + piece, f32),
            jax.ShapeDtypeStruct((heads,) + piece, f32),
        ),
        scratch_shapes=[
            pltpu.VMEM((heads, 2, teams) + piece, bf),
            pltpu.VMEM((2, heads, teams) + piece, bf),
            pltpu.VMEM((heads, 4, 2, r, depth), bf),
            pltpu.VMEM((heads,) + piece, bf),
            pltpu.VMEM((2, heads, 4, 2, r, depth), bf),
            pltpu.VMEM((2, heads) + piece, bf),
            pltpu.VMEM((heads, n) + piece, bf),
            pltpu.VMEM((heads, n) + piece, bf),
            pltpu.VMEM((2, stretches, rows, width), bf),
            pltpu.VMEM((2, stretches, rows, width), bf),
            pltpu.VMEM((stretches, rows, width), bf),
            pltpu.VMEM((stretches, rows, width), f32),
            pltpu.VMEM((stretches, rows, width), bf),
            pltpu.VMEM((stretches, parts, rows // parts, width), bf),
            pltpu.VMEM(small, f32),
            pltpu.VMEM(small, f32),
            pltpu.VMEM((n,) + small, f32),
            pltpu.SemaphoreType.DMA((slots,)),
            pltpu.SemaphoreType.DMA((slots,)),
        ],
        compiler_params=pltpu.CompilerParams(
            collective_id=2, has_side_effects=True, vmem_limit_bytes=67043328
        ),
        name="blocks",
    )(fq, fk, fv, rates, aq, ak, av, shard, gain)


def local_blocks(fq, fk, fv, rates, aq, ak, av, fast_weights, gain):
    stretches, rows, _ = fq.shape
    heads = fast_weights.shape[2]
    shard = jnp.transpose(fast_weights.astype(jnp.bfloat16), (2, 1, 0, 3))
    rate = jnp.transpose(rates.reshape(stretches, rows, heads, 3), (0, 2, 3, 1))[..., None]
    mixed, weights, moment = run_blocks(fq, fk, fv, rate, aq, ak, av, shard, gain[None])
    back = (2, 1, 0, 3)
    return (mixed, jnp.transpose(weights, back), jnp.transpose(moment, back))


def pick(*args):
    stretches, rows, _ = args[0].shape
    r, _, _, depth = args[7].shape
    n, parts = lax.axis_size("aa"), lax.axis_size("ba")
    fits = r % 16 == 0 and n == 8 and depth % AD == 0 and stretches == 2
    fits = fits and 2 * rows == WINDOW and rows % (16 * parts) == 0
    return (local_blocks if fits else local)(*args)


def solution(mesh):
    token = P(None, "aa", "ba")
    hidden = P("aa", None, "ba", None)
    return jax.shard_map(
        pick,
        mesh=mesh,
        in_specs=(token,) * 7 + (hidden, P()),
        out_specs=(P(None, ("aa", "ba"), None), hidden, hidden),
        check_vma=False,
    )
```
